512 devices in a mesh: tm: 32 (over y, x), space: 16 (over z, core).
Axes of the slice: x: 4, y: 8, z: 8, core: 2. Of those that a mesh axis runs over, the one named last changes fastest.
Arguments:
- initial: float32 [64, 64, 128], P('space'), may hold values from -6 to 6
- starts: float32 [32, 64, 64, 128], P('tm', 'space'), may hold values from -6 to 6
- conductivity: float32 [64, 64, 128], P('space'), may hold values from 3e-05 to 0.26
Outputs:
- corrected: float32 [32, 64, 64, 128], P('tm', 'space')
- relaxed: float32 [32, 64, 64, 128], P('tm', 'space')
The draws below stay inside these ranges and needn't reach their ends.
All inputs are finite; a program needn't handle non-finite values.
Results may differ from the reference program's by a relative error of at most 0.000023.
Values sent between devices are 32-bit elements; how exact they have to be, the bound alone decides.
A program may use at most 64 MiB of HBM per device.

```python
import math
import jax
import jax.numpy as jnp
from jax import lax

NY = 64
NX = 128
STEPS = 16
NZ = 64
BLOCKS = 32


def level_of(key, extent, cuts, smallest, largest):
    def one(dim, shards_of):
        steps = jax.random.uniform(jax.random.fold_in(jax.random.fold_in(key, 6), dim), (shards_of,), jnp.float32, smallest / len(cuts), largest / len(cuts))
        return jnp.repeat(jnp.exp(steps), extent[dim] // shards_of).reshape((-1,) + (1,) * (len(extent) - dim - 1))

    gain = one(*cuts[0])
    for cut in cuts[1:]:
        gain = gain * one(*cut)
    return gain


def scatter_about(stream_key, shape, deviation, bound, cuts=(), dtype=jnp.bfloat16):
    entries = deviation * jax.random.normal(stream_key, shape, jnp.float32)
    if cuts:
        entries = entries * level_of(stream_key, shape, cuts, -0.22, 0.18)
    return jnp.clip(entries, -bound, bound).astype(dtype)


def setup_inputs(seed: int = 0) -> dict:
    key_list = jax.random.split(jax.random.key(seed), 4)
    initial = scatter_about(key_list[0], (NZ, NY, NX), 1.0, 6.0, ((0, 16),), jnp.float32)
    starts = scatter_about(key_list[1], (BLOCKS, NZ, NY, NX), 1.0, 6.0, ((0, 32), (1, 16)), jnp.float32)
    conductivity = jnp.clip(jnp.exp(math.log(0.26) - 9.06724 * jax.random.uniform(key_list[2], (NZ, NY, NX), jnp.float32) ** level_of(key_list[2], (NZ, NY, NX), ((0, 16),), -0.2, 0.2)), 2.9999999242136255e-05, 0.26)
    return dict(initial=initial, starts=starts, conductivity=conductivity)


FACE_WEIGHTS = (1.0, 1.0, 0.25, 0.25, 0.25, 0.25)


def neighbours(padded):
    return (padded[2:, 1:-1, 1:-1], padded[:-2, 1:-1, 1:-1], padded[1:-1, 2:, 1:-1], padded[1:-1, :-2, 1:-1], padded[1:-1, 1:-1, 2:], padded[1:-1, 1:-1, :-2])


def advance(current, diffusivity):
    scaled = diffusivity * (1.0 + 0.25 * jnp.tanh(current))
    pad_widths = ((0, 0), (1, 1), (1, 1))
    padded = jnp.pad(current, pad_widths)
    padded_scaled = jnp.pad(scaled, pad_widths)
    centre = padded[1:-1, 1:-1, 1:-1]
    centre_scaled = padded_scaled[1:-1, 1:-1, 1:-1]
    change = jnp.zeros_like(centre)
    for beside, beside_scaled, factor in zip(neighbours(padded), neighbours(padded_scaled), FACE_WEIGHTS):
        change = change + factor * 0.5 * (centre_scaled + beside_scaled) * (beside - centre)
    return centre + change


def reference(initial, starts, conductivity):
    z_pad = ((1, 1), (0, 0), (0, 0))
    cond_padded = jnp.pad(conductivity, z_pad)

    def relax_block(current):
        def single_step(counter, values):
            return advance(jnp.pad(values, z_pad), cond_padded)
        return lax.fori_loop(0, STEPS, single_step, current)

    block_ends = lax.map(relax_block, starts)
    previous = jnp.concatenate([initial[None], block_ends[:-1]], axis=0)
    jump_terms = previous - starts
    damping = 1.0 / (1.0 + STEPS * 3.0 * conductivity)

    def chain_step(carried, jump_now):
        carried = damping * carried + jump_now
        return carried, carried

    _, errors = lax.scan(chain_step, jnp.zeros_like(conductivity), jump_terms)
    corrected = starts + errors
    relaxed = lax.map(relax_block, corrected)
    return corrected, relaxed
```

```python
import functools

import jax
import jax.numpy as jnp
from jax import lax
from jax.experimental import pallas as pl
from jax.experimental.pallas import tpu as pltpu
from jax.sharding import PartitionSpec as P

STEPS = 16
REACH = 1
MESH = pl.DeviceIdType.MESH


def kernel(
    n_tm, n_sp, planes, ny, initial_hbm, starts_hbm, k_hbm, corrected_hbm, relaxed_hbm,
    raw, states, work, k1, k2, ends_all, starts_all, corrected_all, out_buf,
    load_sem, store_sem, halo_send, halo_recv, k_send, k_recv, a2a_send, a2a_recv,
):
    nx = raw.shape[-1]
    slab = planes * ny
    halo = REACH * planes
    depth = halo
    rounds = STEPS // depth
    total = planes + 2 * halo
    groups = ny // 8
    chunk = slab // n_tm
    centre = halo * ny
    i = lax.axis_index("tm")
    s = lax.axis_index("space")

    barrier = pltpu.get_barrier_semaphore()
    partners = []
    for d in range(1, REACH + 1):
        partners += [lax.rem(s + d, n_sp), lax.rem(s + n_sp - d, n_sp)]
    for other in partners:
        pl.semaphore_signal(barrier, inc=1, device_id={"space": other}, device_id_type=MESH)

    @pl.loop(1, n_tm)
    def _(d):
        pl.semaphore_signal(
            barrier, inc=1, device_id={"tm": lax.rem(i + d, n_tm)}, device_id_type=MESH
        )

    loads = [
        pltpu.make_async_copy(source, raw.at[n], load_sem.at[n])
        for n, source in enumerate((starts_hbm.at[0], k_hbm, initial_hbm))
    ]
    for load in loads:
        load.start()
    for load in loads:
        load.wait()

    def gathered(n, p, v):
        return raw[n, p, pl.ds(v, 8, stride=groups), :]

    for p in range(planes):
        for v in range(groups):
            row = p * ny + v * 8
            states[0, centre + row : centre + row + 8, :] = gathered(0, p, v)
            k1[centre + row : centre + row + 8, :] = 0.125 * gathered(1, p, v)
            out_buf[0, row : row + 8, :] = gathered(2, p, v)

    pl.semaphore_wait(barrier, 2 * REACH + n_tm - 1)

    def halo_copies(ref, send, recv):
        copies = []
        for d in range(1, REACH + 1):
            for side, other, start in (
                (0, lax.rem(s + d, n_sp), centre - d * slab),
                (1, lax.rem(s + n_sp - d, n_sp), centre + d * slab),
            ):
                n = 2 * (d - 1) + side
                copies.append(
                    pltpu.make_async_remote_copy(
                        src_ref=ref.at[pl.ds(centre, slab)],
                        dst_ref=ref.at[pl.ds(start, slab)],
                        send_sem=send.at[n],
                        recv_sem=recv.at[n],
                        device_id={"space": other},
                        device_id_type=MESH,
                    )
                )
        return copies

    def state_copies(slot):
        return halo_copies(states.at[slot], halo_send.at[slot], halo_recv.at[slot])

    def scatter_copy(kind, source, target, d):
        return pltpu.make_async_remote_copy(
            src_ref=source,
            dst_ref=target,
            send_sem=a2a_send.at[kind, d],
            recv_sem=a2a_recv.at[kind, d],
            device_id={"tm": lax.rem(i + d, n_tm)},
            device_id_type=MESH,
        )

    def rows_of(index, base=0):
        return pl.ds(pl.multiple_of(base + index * chunk, 8), chunk)

    def starts_copy(d):
        j = lax.rem(i + d, n_tm)
        return scatter_copy(0, states.at[0, rows_of(j, centre)], starts_all.at[rows_of(i)], d)

    def ends_copy(d):
        j = lax.rem(i + d, n_tm)
        return scatter_copy(1, states.at[rounds, rows_of(j, centre)], ends_all.at[rows_of(i)], d)

    def corrected_copy(d):
        j = lax.rem(i + d, n_tm)
        return scatter_copy(
            2, corrected_all.at[rows_of(j)], states.at[rounds + 1, rows_of(i, centre)], d
        )

    def all_partners(action):
        @pl.loop(1, n_tm)
        def _(d):
            action(d)

    k_copies = halo_copies(k1, k_send, k_recv)
    for a, b in zip(k_copies, state_copies(0)):
        a.start()
        b.start()
    all_partners(lambda d: starts_copy(d).start())
    starts_all[rows_of(i), :] = states[0, rows_of(i, centre), :]

    left = [None] + [jnp.where(s >= d, 1.0, 0.0).astype(jnp.float32) for d in range(1, REACH + 1)]
    right = [None] + [
        jnp.where(s + d < n_sp, 1.0, 0.0).astype(jnp.float32) for d in range(1, REACH + 1)
    ]

    def inside(p):
        if p < halo:
            return left[(halo - p + planes - 1) // planes]
        if p >= halo + planes:
            return right[(p - halo) // planes]
        return None

    def edge(p):
        return (p < halo and (halo - 1 - p) % planes == 0) or (
            p >= halo + planes and (p - halo) % planes == 0
        )

    def at(p):
        return slice(p * ny, (p + 1) * ny)

    for a in k_copies:
        a.wait()
    for p in range(total):
        k = k1[at(p), :]
        mask = inside(p)
        if mask is not None:
            k = k * mask
            k1[at(p), :] = k
        k2[at(p), :] = 0.25 * k

    lane = lax.broadcasted_iota(jnp.int32, (ny, nx), 1)
    first_lane = lane == 0
    last_lane = lane == nx - 1
    sublane = lax.broadcasted_iota(jnp.int32, (8, nx), 0)
    first_row = sublane == 0
    last_row = sublane == 7

    def above(x):
        end = jnp.where(last_row, 0.0, pltpu.roll(x[:8], 7, 0))
        return jnp.concatenate([x[8:], end], axis=0)

    def advance(read, write, lo, hi):
        def plane(p):
            u = read(p)
            return u, k1[at(p), :] + k2[at(p), :] * jnp.tanh(u)

        u, a = plane(lo - 1)
        next_u, next_a = plane(lo)
        below = (a + next_a) * (next_u - u)
        for p in range(lo, hi):
            u, a = next_u, next_a
            next_u, next_a = plane(p + 1)
            flux_z = (a + next_a) * (next_u - u)
            flux_y = (a + above(a)) * (above(u) - u)
            own = a * u
            low_y = jnp.concatenate(
                [jnp.where(first_row, own[:8], pltpu.roll(flux_y[-8:], 1, 0)), flux_y[:-8]], axis=0
            )
            beside_u = jnp.where(last_lane, 0.0, pltpu.roll(u, nx - 1, 1))
            beside_a = jnp.where(last_lane, 0.0, pltpu.roll(a, nx - 1, 1))
            flux_x = (a + beside_a) * (beside_u - u)
            low_x = jnp.where(first_lane, own, pltpu.roll(flux_x, 1, 1))
            new = u + (((flux_x - low_x) + (flux_y - low_y)) + 4.0 * (flux_z - below))
            if edge(p):
                new = new * inside(p)
            write(p, new)
            below = flux_z

    def relax_round(slot):
        for t in range(1, depth + 1):

            def read(p, t=t):
                if t > 1:
                    return work[at(p), :]
                u = states[slot, at(p), :]
                mask = inside(p)
                return u if mask is None else u * mask

            def write(p, value, t=t):
                if t < depth:
                    work[at(p), :] = value
                else:
                    states[slot + 1, at(p), :] = value

            advance(read, write, t, total - t)

    def relax(base):
        @pl.loop(0, rounds)
        def _(r):
            slot = base + r
            for copy in state_copies(slot):
                copy.wait()
            relax_round(slot)

            @pl.when(r < rounds - 1)
            def _():
                for copy in state_copies(slot + 1):
                    copy.start()

    relax(0)

    all_partners(lambda d: ends_copy(d).start())
    ends_all[rows_of(i), :] = states[rounds, rows_of(i, centre), :]
    all_partners(lambda d: starts_copy(d).wait())
    all_partners(lambda d: ends_copy(d).wait())

    damping = 1.0 / (1.0 + (STEPS * 3.0 * 8.0) * k1[rows_of(i, centre), :])
    begin = starts_all[0:chunk, :]
    error = out_buf[0, rows_of(i), :] - begin
    corrected_all[0:chunk, :] = begin + error
    for j in range(1, n_tm):
        begin = starts_all[j * chunk : (j + 1) * chunk, :]
        jump = ends_all[(j - 1) * chunk : j * chunk, :] - begin
        error = damping * error + jump
        corrected_all[j * chunk : (j + 1) * chunk, :] = begin + error

    all_partners(lambda d: corrected_copy(d).start())
    states[rounds + 1, rows_of(i, centre), :] = corrected_all[rows_of(i), :]
    all_partners(lambda d: corrected_copy(d).wait())

    for copy in state_copies(rounds + 1):
        copy.start()

    def restore(slot, n, target):
        for p in range(planes):
            for v in range(groups):
                row = centre + p * ny + v * 8
                raw[n, p, pl.ds(v, 8, stride=groups), :] = states[slot, row : row + 8, :]
        copy = pltpu.make_async_copy(raw.at[n], target.at[0], store_sem.at[n])
        copy.start()
        return copy

    first = restore(rounds + 1, 0, corrected_hbm)
    relax(rounds + 1)
    second = restore(2 * rounds + 1, 1, relaxed_hbm)
    first.wait()
    second.wait()


def solution(mesh):
    n_tm, n_sp = mesh.shape["tm"], mesh.shape["space"]

    def on_device(initial, starts, conductivity):
        planes, ny, nx = initial.shape
        slab = planes * ny
        halo = REACH * planes
        total = planes + 2 * halo
        slots = 2 * (STEPS // halo + 1)
        f32 = jnp.float32
        out = jax.ShapeDtypeStruct(starts.shape, f32)
        return pl.pallas_call(
            functools.partial(kernel, n_tm, n_sp, planes, ny),
            out_shape=(out, out),
            in_specs=[pl.BlockSpec(memory_space=pl.ANY)] * 3,
            out_specs=[pl.BlockSpec(memory_space=pl.ANY)] * 2,
            scratch_shapes=[
                pltpu.VMEM((3, planes, ny, nx), f32),
                pltpu.VMEM((slots, total * ny, nx), f32),
                pltpu.VMEM((total * ny, nx), f32),
                pltpu.VMEM((total * ny, nx), f32),
                pltpu.VMEM((total * ny, nx), f32),
                pltpu.VMEM((slab, nx), f32),
                pltpu.VMEM((slab, nx), f32),
                pltpu.VMEM((slab, nx), f32),
                pltpu.VMEM((1, slab, nx), f32),
                pltpu.SemaphoreType.DMA((3,)),
                pltpu.SemaphoreType.DMA((2,)),
                pltpu.SemaphoreType.DMA((slots, 2 * REACH)),
                pltpu.SemaphoreType.DMA((slots, 2 * REACH)),
                pltpu.SemaphoreType.DMA((2 * REACH,)),
                pltpu.SemaphoreType.DMA((2 * REACH,)),
                pltpu.SemaphoreType.DMA((3, n_tm)),
                pltpu.SemaphoreType.DMA((3, n_tm)),
            ],
            compiler_params=pltpu.CompilerParams(collective_id=0, has_side_effects=True),
        )(initial, starts, conductivity)

    in_specs = (P("space", None, None), P("tm", "space", None, None), P("space", None, None))
    out_specs = (P("tm", "space", None, None), P("tm", "space", None, None))
    return jax.shard_map(
        on_device, mesh=mesh, in_specs=in_specs, out_specs=out_specs, check_vma=False
    )
```

```python
import functools

import jax
import jax.numpy as jnp
from jax import lax
from jax.experimental import pallas as pl
from jax.experimental.pallas import tpu as pltpu
from jax.sharding import PartitionSpec as P

STEPS = 16
FAR = 8
NEAR = 4
OWN = 4
ROUNDS = STEPS // FAR
TOTAL = FAR + OWN + NEAR
END = ROUNDS
AGAIN = ROUNDS + 1
LAST = AGAIN + ROUNDS
MESH = pl.DeviceIdType.MESH


def kernel(
    n_tm, n_sp, ny, initial_hbm, starts_hbm, k_hbm, corrected_hbm, relaxed_hbm,
    raw, state, middle, level_u, level_a, k_in, k1, k2,
    ends_all, starts_all, corrected_all, first_all,
    load_sem, store_sem, halo_send, halo_recv, mid_send, mid_recv, a2a_send, a2a_recv,
):
    nx = raw.shape[-1]
    slab = OWN * ny
    groups = ny // 8
    chunk = slab // n_tm
    base = FAR * ny
    i = lax.axis_index("tm")
    s = lax.axis_index("space")
    odd = lax.rem(s, 2)
    turn = 1 - 2 * odd
    facing = lax.rem(s + n_sp - turn, n_sp)
    behind = lax.rem(s + n_sp + 2 * turn, n_sp)
    ahead = lax.rem(s + n_sp - 2 * turn, n_sp)
    sibling = s + turn

    barrier = pltpu.get_barrier_semaphore()
    for other in (facing, behind, ahead, sibling):
        pl.semaphore_signal(barrier, inc=1, device_id={"space": other}, device_id_type=MESH)

    @pl.loop(1, n_tm)
    def _(d):
        pl.semaphore_signal(
            barrier, inc=1, device_id={"tm": lax.rem(i + d, n_tm)}, device_id_type=MESH
        )

    loads = [
        pltpu.make_async_copy(source, raw.at[n], load_sem.at[n])
        for n, source in enumerate((starts_hbm.at[0], k_hbm, initial_hbm))
    ]
    for load in loads:
        load.start()
    for load in loads:
        load.wait()

    lane = lax.broadcasted_iota(jnp.int32, (8, nx), 1)
    sublane = lax.broadcasted_iota(jnp.int32, (8, nx), 0)
    split = (lane % 16) * 8 + (8 - lane // 16) % 8
    flip = (8 - lane // 16) % 8 * 16 + lane % 16
    join = (lane % 8) * 16 + lane // 8

    def permuted(x, index):
        return jnp.take_along_axis(x, index, axis=1)

    def exchanged(x):
        x = pltpu.roll(x, 0, 1, stride=16, stride_axis=0)
        for bit in (1, 2, 4):
            x = jnp.where((lane // 16) & bit != 0, pltpu.roll(x, 8 - bit, 0), x)
        return pltpu.roll(x, 0, 1, stride=16, stride_axis=0)

    def taken_in(x):
        return exchanged(permuted(x, split))

    def given_out(x):
        return permuted(exchanged(permuted(x, flip)), join)

    def raw_rows(n, p, v):
        return n, p * turn + (OWN - 1) * odd, pl.ds(v, 8, stride=groups), slice(None)

    for p in range(OWN):
        for v in range(groups):
            row = p * ny + v * 8
            state[0, base + row : base + row + 8, :] = taken_in(raw[raw_rows(0, p, v)])
            k_in[base + row : base + row + 8, :] = 0.125 * taken_in(raw[raw_rows(1, p, v)])

    pl.semaphore_wait(barrier, 4 + n_tm - 1)

    def planes(p, n=1):
        return pl.ds(p * ny, n * ny)

    def hop(ref, start, stop, n, other, send, recv):
        return pltpu.make_async_remote_copy(
            src_ref=ref.at[planes(start, n)],
            dst_ref=ref.at[planes(stop, n)],
            send_sem=send,
            recv_sem=recv,
            device_id={"space": other},
            device_id_type=MESH,
        )

    def across(ref, q):
        return [
            hop(ref, FAR + p, FAR - 1 - p, 1, facing, halo_send.at[q, p], halo_recv.at[q, p])
            for p in range(OWN)
        ]

    def beyond(ref, q):
        return [
            hop(ref, FAR + p, p, 2, behind, halo_send.at[q, n], halo_recv.at[q, n])
            for n, p in ((4, 2), (5, 0))
        ]

    def beside(ref, send, recv):
        return [
            hop(ref, FAR + p, TOTAL - 1 - p, 1, sibling, send(p), recv(p)) for p in range(OWN)
        ]

    def beside_start(ref, q):
        return beside(ref, lambda p: halo_send.at[q, 6 + p], lambda p: halo_recv.at[q, 6 + p])

    def beside_middle(q):
        return beside(middle.at[q], lambda p: mid_send.at[q, p], lambda p: mid_recv.at[q, p])

    for n in range(chunk // 8):
        part = i * (chunk // 8) + n
        first_all[n * 8 : n * 8 + 8, :] = taken_in(raw[raw_rows(2, part // groups, part % groups)])

    def rows_of(index, start=0):
        return pl.ds(pl.multiple_of(start + index * chunk, 8), chunk)

    def scatter_copy(kind, source, target, d):
        return pltpu.make_async_remote_copy(
            src_ref=source,
            dst_ref=target,
            send_sem=a2a_send.at[kind, d],
            recv_sem=a2a_recv.at[kind, d],
            device_id={"tm": lax.rem(i + d, n_tm)},
            device_id_type=MESH,
        )

    def starts_copy(d):
        j = lax.rem(i + d, n_tm)
        return scatter_copy(0, state.at[0, rows_of(j, base)], starts_all.at[rows_of(i)], d)

    def ends_copy(d):
        j = lax.rem(i + d, n_tm)
        return scatter_copy(1, state.at[END, rows_of(j, base)], ends_all.at[rows_of(i)], d)

    def corrected_copy(d):
        j = lax.rem(i + d, n_tm)
        return scatter_copy(2, corrected_all.at[rows_of(j)], state.at[AGAIN, rows_of(i, base)], d)

    def all_partners(action):
        @pl.loop(1, n_tm)
        def _(d):
            action(d)

    K = LAST + 1
    k_copies = across(k_in, K) + beyond(k_in, K) + beside_start(k_in, K)

    def send_start(slot):
        for copy in beside_start(state.at[slot], slot) + across(state.at[slot], slot):
            copy.start()

    for copy in k_copies:
        copy.start()
    send_start(0)
    all_partners(lambda d: starts_copy(d).start())
    starts_all[rows_of(i), :] = state[0, rows_of(i, base), :]

    end = jnp.where(odd == 0, s == 0, s == n_sp - 1)
    inside = jnp.where(end, 0.0, 1.0).astype(jnp.float32)

    def at(p, v):
        return slice((p + FAR) * ny + v * 8, (p + FAR) * ny + v * 8 + 8)

    for copy in k_copies:
        copy.wait()
    for p in range(-FAR, OWN + NEAR):
        for v in range(groups):
            k = k_in[at(p, v), :]
            if p < 0:
                k = k * inside
            k1[at(p, v), :] = k
            k2[at(p, v), :] = 0.25 * k

    first_x = lane % 16 == 0
    last_x = lane % 16 == 15
    first_y = lane < 16
    last_y = lane >= nx - 16

    def diffusivity(p, v, u):
        return k1[at(p, v), :] + k2[at(p, v), :] * jnp.tanh(u)

    def relax(first_slot):
        @pl.loop(0, ROUNDS)
        def _(r):
            slot = first_slot + r
            q = r + (ROUNDS if first_slot else 0)

            def wide(p, v, shift=0):
                row = ((p + FAR) * groups + v) * 16 + 8 + shift
                return slice(row, row + 8)

            def wide_all(p, shift):
                return pl.ds((p + FAR) * groups * 16 + 8 + shift, 8, stride=16)

            def put(t, p, v, u):
                if t == FAR:
                    state[slot + 1, at(p, v), :] = u
                    return
                level_u[t, wide(p, v), :] = u
                level_a[t, wide(p, v), :] = diffusivity(p, v, u)
                if t == 4 and 0 <= p < OWN:
                    middle[q, at(p, v), :] = u

            def close(t, p):
                if t == FAR:
                    return
                for ref in (level_u, level_a):
                    after = pltpu.roll(ref[t, wide_all(p, 0), :], nx - 1, 1)
                    before = pltpu.roll(ref[t, wide_all(p, 7), :], 1, 1)
                    ref[t, wide_all(p, 8), :] = jnp.where(last_x, 0.0, after)
                    ref[t, wide_all(p, -1), :] = jnp.where(first_x, 0.0, before)

            def ingest(p):
                for v in range(groups):
                    u = state[slot, at(p, v), :]
                    put(0, p, v, u * inside if p < 0 else u)
                close(0, p)

            def strip(t, lo, hi):
                def old(p, v, shift=0):
                    rows = wide(p, v, shift)
                    return level_u[t - 1, rows, :], level_a[t - 1, rows, :]

                def flux(here, there):
                    return (here[1] + there[1]) * (there[0] - here[0])

                below = [None] * groups
                for p in range(lo, hi + 1):
                    cells = [old(p, v) for v in range(groups)]
                    over = tuple(
                        jnp.where(last_y, 0.0, pltpu.roll(x, nx - 16, 1)) for x in cells[0]
                    )
                    top = flux(cells[-1], over)
                    low_y = jnp.where(
                        first_y, cells[0][0] * cells[0][1], pltpu.roll(top, 16, 1)
                    )
                    for v in range(groups):
                        here = cells[v]
                        if p == lo:
                            below[v] = flux(old(p - 1, v), here)
                        flux_z = flux(here, old(p + 1, v))
                        flux_y = top if v == groups - 1 else flux(here, cells[v + 1])
                        flux_x = flux(here, old(p, v, 1)) + flux(here, old(p, v, -1))
                        new = here[0] + (
                            (flux_x + (flux_y - low_y)) + 4.0 * (flux_z - below[v])
                        )
                        if p == -1:
                            new = new * inside
                        put(t, p, v, new)
                        below[v], low_y = flux_z, flux_y
                    close(t, p)

            side, cross, far = (
                beside_start(state.at[slot], slot),
                across(state.at[slot], slot),
                beyond(state.at[slot], slot),
            )
            mid = beside_middle(q)
            for p in range(OWN):
                ingest(p)
            for copy in side:
                copy.wait_recv()
            for copy in far:
                copy.start()
            for p in range(OWN, OWN + NEAR):
                ingest(p)
            strip(1, 1, 6)
            strip(2, 2, 5)
            strip(3, 3, 4)
            for n, arrivals in enumerate((cross[:2], cross[2:], far[:1], far[1:])):
                for copy in arrivals:
                    copy.wait_recv()
                ingest(-1 - 2 * n)
                ingest(-2 - 2 * n)
                for t in range(1, 5):
                    strip(t, t - 2 - 2 * n, t - 1 - 2 * n)
                if n == 0:
                    mid[3].start()
                    mid[2].start()
                if n == 1:
                    mid[1].start()
                    mid[0].start()
            strip(5, -3, 2)
            strip(6, -2, 1)
            strip(7, -1, 0)
            for copy in mid:
                copy.wait_recv()
            for p in range(OWN, OWN + NEAR):
                for v in range(groups):
                    put(4, p, v, middle[q, at(p, v), :])
                close(4, p)
            strip(5, 3, 6)
            strip(6, 2, 5)
            strip(7, 1, 4)
            strip(8, 0, 3)

            @pl.when(r < ROUNDS - 1)
            def _():
                send_start(slot + 1)

            for copy in side + cross + far + mid:
                copy.wait_send()

    relax(0)

    all_partners(lambda d: ends_copy(d).start())
    ends_all[rows_of(i), :] = state[END, rows_of(i, base), :]
    all_partners(lambda d: starts_copy(d).wait())
    all_partners(lambda d: ends_copy(d).wait())

    damping = 1.0 / (1.0 + (STEPS * 3.0 * 8.0) * k_in[rows_of(i, base), :])
    begin = starts_all[0:chunk, :]
    error = first_all[...] - begin
    corrected_all[0:chunk, :] = begin + error
    for j in range(1, n_tm):
        begin = starts_all[j * chunk : (j + 1) * chunk, :]
        jump = ends_all[(j - 1) * chunk : j * chunk, :] - begin
        error = damping * error + jump
        corrected_all[j * chunk : (j + 1) * chunk, :] = begin + error

    all_partners(lambda d: corrected_copy(d).start())
    state[AGAIN, rows_of(i, base), :] = corrected_all[rows_of(i), :]
    all_partners(lambda d: corrected_copy(d).wait())

    send_start(AGAIN)

    def restore(slot, n, target):
        for p in range(OWN):
            for v in range(groups):
                raw[raw_rows(n, p, v)] = given_out(state[slot, at(p, v), :])
        copy = pltpu.make_async_copy(raw.at[n], target.at[0], store_sem.at[n])
        copy.start()
        return copy

    first = restore(AGAIN, 0, corrected_hbm)
    relax(AGAIN)
    second = restore(LAST, 1, relaxed_hbm)
    first.wait()
    second.wait()


def solution(mesh):
    n_tm, n_sp = mesh.shape["tm"], mesh.shape["space"]

    def on_device(initial, starts, conductivity):
        own, ny, nx = initial.shape
        slab = own * ny
        f32 = jnp.float32
        out = jax.ShapeDtypeStruct(starts.shape, f32)
        region = (TOTAL * ny, nx)
        return pl.pallas_call(
            functools.partial(kernel, n_tm, n_sp, ny),
            out_shape=(out, out),
            in_specs=[pl.BlockSpec(memory_space=pl.ANY)] * 3,
            out_specs=[pl.BlockSpec(memory_space=pl.ANY)] * 2,
            scratch_shapes=[
                pltpu.VMEM((3, own, ny, nx), f32),
                pltpu.VMEM((LAST + 1, *region), f32),
                pltpu.VMEM((2 * ROUNDS, *region), f32),
                pltpu.VMEM((FAR, 2 * TOTAL * ny + 8, nx), f32),
                pltpu.VMEM((FAR, 2 * TOTAL * ny + 8, nx), f32),
                pltpu.VMEM(region, f32),
                pltpu.VMEM(region, f32),
                pltpu.VMEM(region, f32),
                pltpu.VMEM((slab, nx), f32),
                pltpu.VMEM((slab, nx), f32),
                pltpu.VMEM((slab, nx), f32),
                pltpu.VMEM((slab // n_tm, nx), f32),
                pltpu.SemaphoreType.DMA((3,)),
                pltpu.SemaphoreType.DMA((2,)),
                pltpu.SemaphoreType.DMA((LAST + 2, 10)),
                pltpu.SemaphoreType.DMA((LAST + 2, 10)),
                pltpu.SemaphoreType.DMA((2 * ROUNDS, OWN)),
                pltpu.SemaphoreType.DMA((2 * ROUNDS, OWN)),
                pltpu.SemaphoreType.DMA((3, n_tm)),
                pltpu.SemaphoreType.DMA((3, n_tm)),
            ],
            compiler_params=pltpu.CompilerParams(collective_id=0, has_side_effects=True),
        )(initial, starts, conductivity)

    in_specs = (P("space", None, None), P("tm", "space", None, None), P("space", None, None))
    out_specs = (P("tm", "space", None, None), P("tm", "space", None, None))
    return jax.shard_map(
        on_device, mesh=mesh, in_specs=in_specs, out_specs=out_specs, check_vma=False
    )
```

```python
import functools

import jax
import jax.numpy as jnp
from jax import lax
from jax.experimental import pallas as pl
from jax.experimental.pallas import tpu as pltpu
from jax.sharding import PartitionSpec as P

STEPS = 16
FAR = 8
NEAR = 4
OWN = 4
ROUNDS = STEPS // FAR
TOTAL = FAR + OWN + NEAR
END = ROUNDS
AGAIN = ROUNDS + 1
LAST = AGAIN + ROUNDS
MESH = pl.DeviceIdType.MESH


def kernel(
    n_tm, n_sp, ny, initial_hbm, starts_hbm, k_hbm, corrected_hbm, relaxed_hbm,
    raw, state, middle, level_u, level_a, k_in, k1, k2,
    ends_all, starts_all, corrected_all, first_all,
    load_sem, store_sem, halo_send, halo_recv, mid_send, mid_recv, a2a_send, a2a_recv,
):
    nx = raw.shape[-1]
    slab = OWN * ny
    groups = ny // 8
    chunk = slab // n_tm
    base = FAR * ny
    i = lax.axis_index("tm")
    n_x = n_tm // 8 if n_tm >= 16 else 2
    n_y = n_tm // n_x
    s = lax.axis_index("space")
    odd = lax.rem(s, 2)
    turn = 1 - 2 * odd
    facing = lax.rem(s + n_sp - turn, n_sp)
    behind = lax.rem(s + n_sp + 2 * turn, n_sp)
    ahead = lax.rem(s + n_sp - 2 * turn, n_sp)
    sibling = s + turn

    barrier = pltpu.get_barrier_semaphore()
    for other in (facing, behind, ahead, sibling):
        pl.semaphore_signal(barrier, inc=1, device_id={"space": other}, device_id_type=MESH)

    @pl.loop(1, n_tm)
    def _(d):
        pl.semaphore_signal(
            barrier, inc=1, device_id={"tm": lax.rem(i + d, n_tm)}, device_id_type=MESH
        )

    loads = [
        pltpu.make_async_copy(source, raw.at[n], load_sem.at[n])
        for n, source in enumerate((starts_hbm.at[0], k_hbm, initial_hbm))
    ]
    for load in loads:
        load.start()
    for load in loads:
        load.wait()

    lane = lax.broadcasted_iota(jnp.int32, (8, nx), 1)
    sublane = lax.broadcasted_iota(jnp.int32, (8, nx), 0)
    split = (lane % 16) * 8 + (8 - lane // 16) % 8
    flip = (8 - lane // 16) % 8 * 16 + lane % 16
    join = (lane % 8) * 16 + lane // 8

    def permuted(x, index):
        return jnp.take_along_axis(x, index, axis=1)

    def exchanged(x):
        x = pltpu.roll(x, 0, 1, stride=16, stride_axis=0)
        for bit in (1, 2, 4):
            x = jnp.where((lane // 16) & bit != 0, pltpu.roll(x, 8 - bit, 0), x)
        return pltpu.roll(x, 0, 1, stride=16, stride_axis=0)

    def taken_in(x):
        return exchanged(permuted(x, split))

    def given_out(x):
        return permuted(exchanged(permuted(x, flip)), join)

    def raw_rows(n, p, v):
        return n, p * turn + (OWN - 1) * odd, pl.ds(v, 8, stride=groups), slice(None)

    for p in range(OWN):
        for v in range(groups):
            row = p * ny + v * 8
            state[0, base + row : base + row + 8, :] = taken_in(raw[raw_rows(0, p, v)])
            k_in[base + row : base + row + 8, :] = 0.125 * taken_in(raw[raw_rows(1, p, v)])

    pl.semaphore_wait(barrier, 4 + n_tm - 1)

    def planes(p, n=1):
        return pl.ds(p * ny, n * ny)

    def hop(ref, start, stop, n, other, send, recv):
        return pltpu.make_async_remote_copy(
            src_ref=ref.at[planes(start, n)],
            dst_ref=ref.at[planes(stop, n)],
            send_sem=send,
            recv_sem=recv,
            device_id={"space": other},
            device_id_type=MESH,
        )

    def across(ref, q):
        return [
            hop(ref, FAR + p, FAR - 1 - p, 1, facing, halo_send.at[q, p], halo_recv.at[q, p])
            for p in range(OWN)
        ]

    def beyond(ref, q):
        return [
            hop(ref, FAR + p, p, 2, behind, halo_send.at[q, n], halo_recv.at[q, n])
            for n, p in ((4, 2), (5, 0))
        ]

    def beside(ref, send, recv):
        return [
            hop(ref, FAR + p, TOTAL - 1 - p, 1, sibling, send(p), recv(p)) for p in range(OWN)
        ]

    def beside_start(ref, q):
        return beside(ref, lambda p: halo_send.at[q, 6 + p], lambda p: halo_recv.at[q, 6 + p])

    def beside_middle(q):
        return beside(middle.at[q], lambda p: mid_send.at[q, p], lambda p: mid_recv.at[q, p])

    for n in range(chunk // 8):
        part = i * (chunk // 8) + n
        first_all[n * 8 : n * 8 + 8, :] = taken_in(raw[raw_rows(2, part // groups, part % groups)])

    def rows_of(index, start=0):
        return pl.ds(pl.multiple_of(start + index * chunk, 8), chunk)

    def outward(n, size):
        return size // 2 + (n + 1) // 2 * (1 - 2 * lax.rem(n, 2))

    def partner(d):
        y = lax.rem(i // n_x + outward(d // n_x, n_y), n_y)
        x = lax.rem(lax.rem(i, n_x) + outward(lax.rem(d, n_x), n_x), n_x)
        return y * n_x + x

    def scatter_copy(kind, source, target, d):
        return pltpu.make_async_remote_copy(
            src_ref=source,
            dst_ref=target,
            send_sem=a2a_send.at[kind, d],
            recv_sem=a2a_recv.at[kind, d],
            device_id={"tm": partner(d)},
            device_id_type=MESH,
        )

    def starts_copy(d):
        j = partner(d)
        return scatter_copy(0, state.at[0, rows_of(j, base)], starts_all.at[rows_of(i)], d)

    def ends_copy(d):
        j = partner(d)
        return scatter_copy(1, state.at[END, rows_of(j, base)], ends_all.at[rows_of(i)], d)

    def corrected_copy(d):
        j = partner(d)
        return scatter_copy(2, corrected_all.at[rows_of(j)], state.at[AGAIN, rows_of(i, base)], d)

    def all_partners(action):
        @pl.loop(0, n_tm - 1)
        def _(d):
            action(d)

    K = LAST + 1
    k_copies = across(k_in, K) + beyond(k_in, K) + beside_start(k_in, K)

    def send_start(slot):
        for copy in across(state.at[slot], slot) + beside_start(state.at[slot], slot) + beyond(state.at[slot], slot):
            copy.start()

    for copy in k_copies:
        copy.start()
    send_start(0)
    all_partners(lambda d: starts_copy(d).start())
    starts_all[rows_of(i), :] = state[0, rows_of(i, base), :]

    end = jnp.where(odd == 0, s == 0, s == n_sp - 1)
    inside = jnp.where(end, 0.0, 1.0).astype(jnp.float32)

    def at(p, v):
        return slice((p + FAR) * ny + v * 8, (p + FAR) * ny + v * 8 + 8)

    for copy in k_copies:
        copy.wait()
    for p in range(-FAR, OWN + NEAR):
        for v in range(groups):
            k = k_in[at(p, v), :]
            if p < 0:
                k = k * inside
            k1[at(p, v), :] = k
            k2[at(p, v), :] = 0.25 * k

    first_x = lane % 16 == 0
    last_x = lane % 16 == 15
    first_y = lane < 16
    last_y = lane >= nx - 16

    def diffusivity(p, v, u):
        return k1[at(p, v), :] + k2[at(p, v), :] * jnp.tanh(u)

    def relax(first_slot):
        @pl.loop(0, ROUNDS)
        def _(r):
            slot = first_slot + r
            q = r + (ROUNDS if first_slot else 0)

            def wide(p, v, shift=0):
                row = ((p + FAR) * groups + v) * 16 + 8 + shift
                return slice(row, row + 8)

            def wide_all(p, shift):
                return pl.ds((p + FAR) * groups * 16 + 8 + shift, 8, stride=16)

            def put(t, p, v, u):
                if t == FAR:
                    state[slot + 1, at(p, v), :] = u
                    return
                level_u[t, wide(p, v), :] = u
                level_a[t, wide(p, v), :] = diffusivity(p, v, u)
                if t == 4 and 0 <= p < OWN:
                    middle[q, at(p, v), :] = u

            def close(t, p):
                if t == FAR:
                    return
                for ref in (level_u, level_a):
                    after = pltpu.roll(ref[t, wide_all(p, 0), :], nx - 1, 1)
                    before = pltpu.roll(ref[t, wide_all(p, 7), :], 1, 1)
                    ref[t, wide_all(p, 8), :] = jnp.where(last_x, 0.0, after)
                    ref[t, wide_all(p, -1), :] = jnp.where(first_x, 0.0, before)

            def ingest(p):
                for v in range(groups):
                    u = state[slot, at(p, v), :]
                    put(0, p, v, u * inside if p < 0 else u)
                close(0, p)

            def strip(t, lo, hi):
                def old(p, v, shift=0):
                    rows = wide(p, v, shift)
                    return level_u[t - 1, rows, :], level_a[t - 1, rows, :]

                def flux(here, there):
                    return (here[1] + there[1]) * (there[0] - here[0])

                below = [None] * groups
                for p in range(lo, hi + 1):
                    cells = [old(p, v) for v in range(groups)]
                    over = tuple(
                        jnp.where(last_y, 0.0, pltpu.roll(x, nx - 16, 1)) for x in cells[0]
                    )
                    top = flux(cells[-1], over)
                    low_y = jnp.where(
                        first_y, cells[0][0] * cells[0][1], pltpu.roll(top, 16, 1)
                    )
                    for v in range(groups):
                        here = cells[v]
                        if p == lo:
                            below[v] = flux(old(p - 1, v), here)
                        flux_z = flux(here, old(p + 1, v))
                        flux_y = top if v == groups - 1 else flux(here, cells[v + 1])
                        flux_x = flux(here, old(p, v, 1)) + flux(here, old(p, v, -1))
                        new = here[0] + (
                            (flux_x + (flux_y - low_y)) + 4.0 * (flux_z - below[v])
                        )
                        if p == -1:
                            new = new * inside
                        put(t, p, v, new)
                        below[v], low_y = flux_z, flux_y
                    close(t, p)

            side, cross, far = (
                beside_start(state.at[slot], slot),
                across(state.at[slot], slot),
                beyond(state.at[slot], slot),
            )
            mid = beside_middle(q)
            for p in range(OWN):
                ingest(p)
            for copy in side:
                copy.wait_recv()
            for p in range(OWN, OWN + NEAR):
                ingest(p)
            strip(1, 1, 6)
            strip(2, 2, 5)
            strip(3, 3, 4)
            for n, arrivals in enumerate((cross[:2], cross[2:], far[:1], far[1:])):
                for copy in arrivals:
                    copy.wait_recv()
                ingest(-1 - 2 * n)
                ingest(-2 - 2 * n)
                for t in range(1, 5):
                    strip(t, t - 2 - 2 * n, t - 1 - 2 * n)
                if n == 0:
                    mid[3].start()
                    mid[2].start()
                if n == 1:
                    mid[1].start()
                    mid[0].start()
            strip(5, -3, 2)
            strip(6, -2, 1)
            strip(7, -1, 0)
            for copy in mid:
                copy.wait_recv()
            for p in range(OWN, OWN + NEAR):
                for v in range(groups):
                    put(4, p, v, middle[q, at(p, v), :])
                close(4, p)
            strip(5, 3, 6)
            strip(6, 2, 5)
            strip(7, 1, 4)
            strip(8, 0, 3)

            @pl.when(r < ROUNDS - 1)
            def _():
                send_start(slot + 1)

            for copy in side + cross + far + mid:
                copy.wait_send()

    relax(0)

    all_partners(lambda d: ends_copy(d).start())
    ends_all[rows_of(i), :] = state[END, rows_of(i, base), :]
    all_partners(lambda d: starts_copy(d).wait())
    all_partners(lambda d: ends_copy(d).wait())

    damping = 1.0 / (1.0 + (STEPS * 3.0 * 8.0) * k_in[rows_of(i, base), :])
    begin = starts_all[0:chunk, :]
    error = first_all[...] - begin
    corrected_all[0:chunk, :] = begin + error
    for j in range(1, n_tm):
        begin = starts_all[j * chunk : (j + 1) * chunk, :]
        jump = ends_all[(j - 1) * chunk : j * chunk, :] - begin
        error = damping * error + jump
        corrected_all[j * chunk : (j + 1) * chunk, :] = begin + error

    all_partners(lambda d: corrected_copy(d).start())
    state[AGAIN, rows_of(i, base), :] = corrected_all[rows_of(i), :]
    all_partners(lambda d: corrected_copy(d).wait())

    send_start(AGAIN)

    def restore(slot, n, target):
        for p in range(OWN):
            for v in range(groups):
                raw[raw_rows(n, p, v)] = given_out(state[slot, at(p, v), :])
        copy = pltpu.make_async_copy(raw.at[n], target.at[0], store_sem.at[n])
        copy.start()
        return copy

    first = restore(AGAIN, 0, corrected_hbm)
    relax(AGAIN)
    second = restore(LAST, 1, relaxed_hbm)
    first.wait()
    second.wait()


def solution(mesh):
    n_tm, n_sp = mesh.shape["tm"], mesh.shape["space"]

    def on_device(initial, starts, conductivity):
        own, ny, nx = initial.shape
        slab = own * ny
        f32 = jnp.float32
        out = jax.ShapeDtypeStruct(starts.shape, f32)
        region = (TOTAL * ny, nx)
        return pl.pallas_call(
            functools.partial(kernel, n_tm, n_sp, ny),
            out_shape=(out, out),
            in_specs=[pl.BlockSpec(memory_space=pl.ANY)] * 3,
            out_specs=[pl.BlockSpec(memory_space=pl.ANY)] * 2,
            scratch_shapes=[
                pltpu.VMEM((3, own, ny, nx), f32),
                pltpu.VMEM((LAST + 1, *region), f32),
                pltpu.VMEM((2 * ROUNDS, *region), f32),
                pltpu.VMEM((FAR, 2 * TOTAL * ny + 8, nx), f32),
                pltpu.VMEM((FAR, 2 * TOTAL * ny + 8, nx), f32),
                pltpu.VMEM(region, f32),
                pltpu.VMEM(region, f32),
                pltpu.VMEM(region, f32),
                pltpu.VMEM((slab, nx), f32),
                pltpu.VMEM((slab, nx), f32),
                pltpu.VMEM((slab, nx), f32),
                pltpu.VMEM((slab // n_tm, nx), f32),
                pltpu.SemaphoreType.DMA((3,)),
                pltpu.SemaphoreType.DMA((2,)),
                pltpu.SemaphoreType.DMA((LAST + 2, 10)),
                pltpu.SemaphoreType.DMA((LAST + 2, 10)),
                pltpu.SemaphoreType.DMA((2 * ROUNDS, OWN)),
                pltpu.SemaphoreType.DMA((2 * ROUNDS, OWN)),
                pltpu.SemaphoreType.DMA((3, n_tm)),
                pltpu.SemaphoreType.DMA((3, n_tm)),
            ],
            compiler_params=pltpu.CompilerParams(collective_id=0, has_side_effects=True),
        )(initial, starts, conductivity)

    in_specs = (P("space", None, None), P("tm", "space", None, None), P("space", None, None))
    out_specs = (P("tm", "space", None, None), P("tm", "space", None, None))
    return jax.shard_map(
        on_device, mesh=mesh, in_specs=in_specs, out_specs=out_specs, check_vma=False
    )
```
